32 devices in a mesh: groups: 2 (over y), tiles: 4 (over z), heads: 2 (over x), kv: 2 (over core).
Axes of the slice: x: 2, y: 2, z: 4, core: 2. Of those that a mesh axis runs over, the one named last changes fastest.
Arguments:
- features: bfloat16 [12288, 1536], P(('groups', 'tiles')), parts along dimension 0, may hold values from -6 to 6
- counts: int32 [8], P(('groups', 'tiles')), parts along dimension 0, may hold values from 1 to 6
- tile_mask: int32 [48, 256], P(('groups', 'tiles')), parts along dimension 0, may hold values from 0 to 1, as said below
- queries: bfloat16 [256, 768], P(('heads', 'kv')), may hold values from -6 to 6
- norm_gain: float32 [2, 768], replicated, may hold values from 0.5 to 1.5
- head_scale: float32 [12], P('heads'), may hold values from 1 to 4
- w_query: bfloat16 [2, 768, 768], P(None, None, ('heads', 'kv')), may hold values from -0.21875 to 0.21875
- w_kv: bfloat16 [2, 1536, 2, 768], P(None, None, 'kv', 'heads'), may hold values from -0.15625 to 0.15625
- w_out: bfloat16 [2, 768, 768], P(None, ('heads', 'kv')), may hold values from -0.21875 to 0.21875
Outputs:
- query_states: float32 [512, 768], P(('groups', 'heads', 'kv')), parts along dimension 0
The draws below stay inside these ranges and needn't reach their ends.
There are 2 independent parts, one for each index of `groups`. The reference program is written for one: setup_inputs(seed, part) draws one part's arguments, and reference() takes and returns one part's arrays. A program takes and returns all parts, laid end to end along the dimension named above; an argument that names none is the same for every part. Nothing has to cross between parts.
Inputs may be any that keep to these rules, and one draw needn't show every extreme that they name: `tile_mask`: the first tile of every block slot is 1.
All inputs are finite; a program needn't handle non-finite values.
Results may differ from the reference program's by a relative error of at most 0.012.
The reference program's roundings to bfloat16 on the way count: a program that leaves them out, or rounds other values in their place, can miss the bound.
Values may be sent and summed in bfloat16 or wider, within the bound.
A program may use at most 64 MiB of HBM per device.

```python
import math
import jax
import jax.numpy as jnp
from jax import lax

FEAT = 1536
NQ = 256
NH = 12
HD = 64
LAYERS = 2
BLK = 256
SLOTS = 6
DQ = 768
TILES = 6144
N_TILES = 4


def draw_tile_mask(key, part):
    marks = jax.random.randint(jax.random.fold_in(key, 11), (TILES // BLK, BLK), 0, 4)
    filled = (marks > 0).astype(jnp.int32)
    leading = (jnp.arange(BLK, dtype=jnp.int32) == 0)[None, :]
    return jnp.where(leading, 1, filled).astype(jnp.int32)


def place_ends(values, rng, least, top_value):
    place = [jax.random.randint(jax.random.fold_in(rng, axis), (), 0, length) for axis, length in enumerate(values.shape)]
    longest = values.shape.index(max(values.shape))
    neighbour = place[:longest] + [(place[longest] + 1) % values.shape[longest]] + place[longest + 1:]
    return values.at[tuple(place)].set(least).at[tuple(neighbour)].set(top_value)


def block_levels(stream_key, dims, cuts, low, largest):
    def one(position, parts):
        heights = jax.random.uniform(jax.random.fold_in(jax.random.fold_in(stream_key, 6), position), (parts,), jnp.float32, low / len(cuts), largest / len(cuts))
        return jnp.repeat(jnp.exp(heights), dims[position] // parts).reshape((-1,) + (1,) * (len(dims) - position - 1))

    gain = one(*cuts[0])
    for cut in cuts[1:]:
        gain = gain * one(*cut)
    return gain


def gaussian(own_key, extent, scale, limit, shards=(), held_as=jnp.bfloat16):
    level = block_levels(own_key, extent, shards, -0.22, 0.18) if shards else 1.0
    result = jax.random.normal(own_key, extent, jnp.float32) * scale * level
    return jnp.minimum(jnp.maximum(result, -limit), limit).astype(held_as)


def setup_inputs(seed: int = 0, part: int = 0) -> dict:
    seeds = jax.random.split(jax.random.key(seed), 10)
    part_splits = jax.random.split(jax.random.fold_in(seeds[9], part), 10)
    features = gaussian(part_splits[0], (TILES, FEAT), 1.0, 6.0, ((0, 4),))
    counts = place_ends(jax.random.randint(part_splits[1], (N_TILES,), 1, SLOTS + 1), jax.random.fold_in(part_splits[1], 1), 1, SLOTS).astype(jnp.int32)
    tile_mask = draw_tile_mask(jax.random.fold_in(jax.random.fold_in(seeds[9], part), 71), part)
    queries = gaussian(seeds[3], (NQ, DQ), 1.0, 6.0, ((0, 4),))
    norm_gain = jnp.clip(1.0 + 0.1 * jax.random.normal(seeds[4], (LAYERS, DQ), jnp.float32), 0.5, 1.5)
    head_scale = jnp.clip(jnp.exp(math.log(4.0) - 1.3862944 * jax.random.uniform(seeds[5], (NH,), jnp.float32) ** block_levels(seeds[5], (NH,), ((0, 2),), -0.2, 0.2)), 1.0, 4.0)
    w_query = gaussian(seeds[6], (LAYERS, DQ, DQ), DQ ** -0.5, 0.21875, ((2, 4),))
    w_kv = gaussian(seeds[7], (LAYERS, FEAT, 2, DQ), FEAT ** -0.5, 0.15625, ((2, 2), (3, 2)))
    w_out = gaussian(seeds[8], (LAYERS, DQ, DQ), DQ ** -0.5, 0.21875, ((1, 4),))
    return dict(features=features, counts=counts, tile_mask=tile_mask, queries=queries, norm_gain=norm_gain, head_scale=head_scale, w_query=w_query, w_kv=w_kv, w_out=w_out)


SOFT_CAP = 50.0
NORM_EPS = 1e-06

def normalize(hidden, gain_row):
    return hidden * jax.lax.rsqrt(lax.optimization_barrier(jnp.mean(hidden * hidden, axis=-1, keepdims=True)) + NORM_EPS) * gain_row

def reference(features, counts, tile_mask, queries, norm_gain, head_scale, w_query, w_kv, w_out):
    block_ids = jnp.arange(TILES // BLK, dtype=jnp.int32)
    live_slots = (block_ids % SLOTS < jnp.repeat(counts, SLOTS)).astype(jnp.int32)
    valid_tiles = (tile_mask * live_slots[:, None]).reshape(TILES).astype(jnp.float32)
    states = queries.astype(jnp.float32)
    for layer_at in range(LAYERS):
        normed = normalize(states, norm_gain[layer_at]).astype(jnp.bfloat16)
        query_all = jnp.dot(normed, w_query[layer_at], preferred_element_type=jnp.float32).astype(jnp.bfloat16)
        keys = jnp.dot(features, w_kv[layer_at, :, 0, :], preferred_element_type=jnp.float32).astype(jnp.bfloat16)
        values = jnp.dot(features, w_kv[layer_at, :, 1, :], preferred_element_type=jnp.float32).astype(jnp.bfloat16)
        pieces = []
        for head_at in range(NH):
            low = head_at * HD
            scores = jnp.dot(query_all[:, low:low + HD], keys[:, low:low + HD].T, preferred_element_type=jnp.float32)
            scores = scores * (head_scale[head_at] / math.sqrt(HD))
            capped = SOFT_CAP * jnp.tanh(scores / SOFT_CAP)
            weights = jnp.exp(capped) * valid_tiles[None, :]
            totals = lax.optimization_barrier(jnp.sum(weights, axis=1, keepdims=True))
            partial_value = jnp.dot(weights.astype(jnp.bfloat16), values[:, low:low + HD], preferred_element_type=jnp.float32)
            pieces.append(partial_value / totals)
        attended = jnp.concatenate(pieces, axis=1).astype(jnp.bfloat16)
        states = states + jnp.dot(attended, w_out[layer_at], preferred_element_type=jnp.float32)
    return states
```

```python
import functools
import math

import jax
import jax.numpy as jnp
from jax import lax
from jax.experimental import pallas as pl
from jax.experimental.pallas import tpu as pltpu
from jax.sharding import PartitionSpec as P

SOFT_CAP = 50.0
NORM_EPS = 1e-06


def normalize(hidden, gain_row):
    return (
        hidden * lax.rsqrt(jnp.mean(hidden * hidden, axis=-1, keepdims=True) + NORM_EPS) * gain_row
    )


def body(features, counts, tile_mask, queries, norm_gain, head_scale, w_query, w_kv, w_out):
    slot_count = tile_mask.shape[0]
    block_rows = tile_mask.shape[1]
    total_rows = slot_count * block_rows
    half_rows = total_rows // 2
    layer_count = w_kv.shape[0]
    head_cols = w_kv.shape[3]
    heads_local = head_scale.shape[0]
    head_dim = head_cols // heads_local
    kv_side = lax.axis_index("kv")
    kv_weights = w_kv[:, :, 0, :]
    slot_ids = jnp.arange(slot_count, dtype=jnp.int32)

    def add_block(slot_at, current):
        block_feats = lax.dynamic_slice_in_dim(features, slot_at * block_rows, block_rows, 0)
        result = jnp.einsum(
            "rf,lfc->lrc", block_feats, kv_weights, preferred_element_type=jnp.float32
        )
        return lax.dynamic_update_slice_in_dim(
            current, result.astype(jnp.bfloat16), slot_at * block_rows, 1
        )

    own_count = counts[0]
    projected = jnp.zeros((layer_count, total_rows, head_cols), jnp.bfloat16)
    projected = lax.fori_loop(jnp.int32(0), own_count, add_block, projected)
    live_mask = tile_mask * (slot_ids < own_count).astype(jnp.int32)[:, None]
    kv_local = lax.all_to_all(projected, "kv", split_axis=1, concat_axis=2, tiled=True)
    valid_tiles = lax.dynamic_slice_in_dim(
        live_mask.reshape(total_rows).astype(jnp.float32), kv_side * half_rows, half_rows, 0
    )
    states = queries.astype(jnp.float32)
    scale_vec = head_scale / math.sqrt(head_dim)
    for layer_at in range(layer_count):
        normed = lax.all_gather(
            normalize(states, norm_gain[layer_at]).astype(jnp.bfloat16),
            ("heads", "kv"),
            axis=0,
            tiled=True,
        )
        query_part = jnp.dot(normed, w_query[layer_at], preferred_element_type=jnp.float32).astype(
            jnp.bfloat16
        )
        query_cols = lax.all_gather(query_part, "kv", axis=1, tiled=True)
        n_queries = query_cols.shape[0]
        query_heads = query_cols.reshape(n_queries, heads_local, head_dim)
        key_heads = kv_local[layer_at, :, :head_cols].reshape(half_rows, heads_local, head_dim)
        value_heads = kv_local[layer_at, :, head_cols:].reshape(half_rows, heads_local, head_dim)
        scores = jnp.einsum(
            "qhd,khd->hqk", query_heads, key_heads, preferred_element_type=jnp.float32
        )
        scores = scores * scale_vec[:, None, None]
        capped = SOFT_CAP * jnp.tanh(scores / SOFT_CAP)
        weights_p = jnp.exp(capped) * valid_tiles[None, None, :]
        totals = jnp.sum(weights_p, axis=2)
        partial_value = jnp.einsum(
            "hqk,khd->qhd",
            weights_p.astype(jnp.bfloat16),
            value_heads,
            preferred_element_type=jnp.float32,
        )
        totals, partial_value = lax.psum((totals, partial_value), ("tiles", "kv"))
        attended = (
            (partial_value / jnp.transpose(totals)[:, :, None])
            .reshape(n_queries, head_cols)
            .astype(jnp.bfloat16)
        )
        own_cols = lax.dynamic_slice_in_dim(attended, kv_side * (head_cols // 2), head_cols // 2, 1)
        states = states + lax.psum_scatter(
            jnp.dot(own_cols, w_out[layer_at], preferred_element_type=jnp.float32),
            ("heads", "kv"),
            scatter_dimension=0,
            tiled=True,
        )
    return states


MESH = pl.DeviceIdType.MESH


def fused_kernel(
    n_tiles,
    n_heads,
    n_kv,
    counts_ref,
    scale_ref,
    mask_ref,
    gain_ref,
    features,
    queries,
    w_query,
    w_kv,
    w_out,
    out_ref,
    feat_buf,
    kvw_buf,
    wq_buf,
    wout_buf,
    q_buf,
    kv_buf,
    kv_out,
    valid_buf,
    query_buf,
    acc_buf,
    tot_buf,
    part_buf,
    rs_buf,
    att_buf,
    attz_buf,
    fin_buf,
    load_sem,
    feat_sem,
    own_sem,
    share_send,
    share_recv,
    relay_send,
    relay_recv,
    kv_send,
    kv_recv,
    rs_send,
    rs_recv,
    att_send,
    att_recv,
    qry_send,
    qry_recv,
    attz_send,
    attz_recv,
    fin_send,
    fin_recv,
):
    tile_at = lax.axis_index("tiles")
    head_at = lax.axis_index("heads")
    kv_at = lax.axis_index("kv")
    members = n_heads * n_kv
    member = head_at * n_kv + kv_at
    slots, block, _ = feat_buf.shape
    layers = wq_buf.shape[0]
    cols = wq_buf.shape[2]
    width = rs_buf.shape[3]
    own_heads = acc_buf.shape[0]
    head_dim = acc_buf.shape[2]
    n_queries, dq = q_buf.shape
    tile_rows = n_queries // n_tiles
    own_rows = n_queries // members
    side_cols = w_kv.shape[2]

    def tile_peer(step):
        return {"tiles": lax.rem(tile_at + step, n_tiles)}

    def member_peer(step):
        other = lax.rem(member + step, members)
        return {"heads": other // n_kv, "kv": lax.rem(other, n_kv)}

    def remote(src, dst, send, recv, where):
        return pltpu.make_async_remote_copy(
            src_ref=src,
            dst_ref=dst,
            send_sem=send,
            recv_sem=recv,
            device_id=where,
            device_id_type=MESH,
        )

    barrier = pltpu.get_barrier_semaphore()
    for step in range(1, n_tiles):
        pl.semaphore_signal(barrier, inc=1, device_id=tile_peer(step), device_id_type=MESH)
    for step in range(1, members):
        pl.semaphore_signal(barrier, inc=1, device_id=member_peer(step), device_id_type=MESH)

    loads = [
        pltpu.make_async_copy(
            w_kv.at[layer],
            kvw_buf.at[:, pl.ds(layer * side_cols, side_cols)],
            load_sem.at[layer],
        )
        for layer in range(layers)
    ]
    feat_loads = [
        pltpu.make_async_copy(
            features.at[pl.ds(slot * block, block)], feat_buf.at[slot], feat_sem.at[slot]
        )
        for slot in range(slots)
    ]
    wq_load = pltpu.make_async_copy(w_query, wq_buf, load_sem.at[layers])
    for copy in loads[:1] + feat_loads[:1] + loads[1:] + feat_loads[1:]:
        copy.start()
    wq_load.start()
    own_q = pltpu.make_async_copy(
        queries, q_buf.at[pl.ds(member * own_rows, own_rows)], own_sem.at[0]
    )
    own_w = [
        pltpu.make_async_copy(w_out.at[layer], wout_buf.at[layer, member], own_sem.at[1 + layer])
        for layer in range(layers)
    ]
    own_q.start()
    for copy in own_w:
        copy.start()

    pl.semaphore_wait(barrier, n_tiles - 1 + members - 1)

    def item_at(item, owner):
        if item == 0:
            return q_buf.at[pl.ds(owner * own_rows, own_rows)]
        return wout_buf.at[item - 1, owner]

    sources = [queries] + [w_out.at[layer] for layer in range(layers)]
    items = range(len(sources))
    shares = {}
    for item in items:
        for hop in range(1, n_heads):
            shares[item, hop] = remote(
                sources[item],
                item_at(item, member),
                share_send.at[item, hop],
                share_recv.at[item, hop],
                {"heads": lax.rem(head_at + hop, n_heads)},
            )
            shares[item, hop].start()
    relays = {}

    def start_relay(item, hop):
        owner = lax.rem(head_at - hop + n_heads, n_heads) * n_kv + kv_at
        src = sources[item] if hop == 0 else item_at(item, owner)
        relays[item, hop] = remote(
            src,
            item_at(item, owner),
            relay_send.at[item, hop],
            relay_recv.at[item, hop],
            {"kv": lax.rem(kv_at + 1, n_kv)},
        )
        relays[item, hop].start()

    def finish_item(item):
        for hop in range(n_heads):
            relays[item, hop].wait()

    for item in items:
        start_relay(item, 0)

    live = lax.broadcasted_iota(jnp.int32, mask_ref.shape, 0) < counts_ref[0]
    valid_buf[...] = jnp.where(live, mask_ref[...], 0).astype(jnp.float32)

    def kv_copy(slot):
        return remote(
            kv_out.at[slot],
            kv_buf.at[slot, kv_at],
            kv_send.at[slot],
            kv_recv.at[slot],
            {"kv": lax.rem(kv_at + 1, n_kv)},
        )

    for copy in loads:
        copy.wait()

    def project(slot, carry):
        pltpu.make_async_copy(
            features.at[pl.ds(0, block)], feat_buf.at[slot], feat_sem.at[slot]
        ).wait()
        rows = jnp.dot(feat_buf[slot], kvw_buf[...], preferred_element_type=jnp.float32)
        for layer in range(layers):
            at = layer * side_cols
            low = rows[:, at : at + cols]
            high = rows[:, at + cols : at + 2 * cols]
            first = kv_at == 0
            kv_buf[slot, kv_at, layer] = jnp.where(first, low, high).astype(jnp.bfloat16)
            kv_out[slot, layer] = jnp.where(first, high, low).astype(jnp.bfloat16)
        kv_copy(slot).start()
        return carry

    lax.fori_loop(0, slots, project, 0)

    own_q.wait()
    for hop in range(1, n_heads):
        shares[0, hop].wait()
        start_relay(0, hop)
    finish_item(0)
    wq_load.wait()

    def to_query(states, layer):
        normed = normalize(states, gain_ref[pl.ds(layer, 1)]).astype(jnp.bfloat16)
        return jnp.dot(normed, wq_buf[layer], preferred_element_type=jnp.float32).astype(
            jnp.bfloat16
        )

    query_buf[0] = to_query(q_buf[...].astype(jnp.float32), 0)
    own_w[0].wait()
    for hop in range(1, n_heads):
        shares[1, hop].wait()
        start_relay(1, hop)

    def attend(layer):
        acc_buf[...] = jnp.zeros_like(acc_buf)
        tot_buf[...] = jnp.zeros_like(tot_buf)
        lanes = tot_buf.shape[2]

        def add_block(slot, carry):
            if layer == 0:
                kv_copy(slot).wait_recv()
            valid_row = valid_buf[pl.ds(slot, 1)]
            for at in range(own_heads):
                low, high = at * head_dim, (at + 1) * head_dim
                scale = scale_ref[kv_at * own_heads + at] * (
                    1.0 / (math.sqrt(head_dim) * SOFT_CAP)
                )
                scores = lax.dot_general(
                    query_buf[layer, :, low:high],
                    kv_buf[slot, 0, layer, :, low:high],
                    (((1,), (1,)), ((), ())),
                    preferred_element_type=jnp.float32,
                )
                weights = jnp.exp(SOFT_CAP * jnp.tanh(scores * scale)) * valid_row
                total = weights[:, :lanes]
                for part in range(1, block // lanes):
                    total = total + weights[:, part * lanes : (part + 1) * lanes]
                tot_buf[at] += total
                acc_buf[at] += jnp.dot(
                    weights.astype(jnp.bfloat16),
                    kv_buf[slot, 1, layer, :, low:high],
                    preferred_element_type=jnp.float32,
                )
            return carry

        lax.fori_loop(0, slots, add_block, 0)
        tail_width = width - cols
        lane = lax.broadcasted_iota(jnp.int32, (n_queries, tail_width), 1)
        tail = jnp.zeros((n_queries, tail_width), jnp.float32)
        for at in range(own_heads):
            part_buf[layer, :, at * head_dim : (at + 1) * head_dim] = acc_buf[at].astype(
                jnp.bfloat16
            )
            total = jnp.sum(tot_buf[at], axis=1, keepdims=True)
            coarse = total.astype(jnp.bfloat16).astype(jnp.float32)
            tail = jnp.where(lane == at, coarse, tail)
            tail = jnp.where(lane == own_heads + at, total - coarse, tail)
        part_buf[layer, :, cols:width] = tail.astype(jnp.bfloat16)
        copies = []
        for step in range(1, n_tiles):
            other = lax.rem(tile_at + step, n_tiles)
            copies.append(
                remote(
                    part_buf.at[layer, pl.ds(other * tile_rows, tile_rows)],
                    rs_buf.at[layer, tile_at],
                    rs_send.at[layer, step],
                    rs_recv.at[layer, step],
                    tile_peer(step),
                )
            )
            copies[-1].start()
        return copies

    def merge(layer, copies):
        own = part_buf[layer, pl.ds(tile_at * tile_rows, tile_rows)].astype(jnp.float32)
        for step in range(1, n_tiles):
            copies[step - 1].wait()
            other = lax.rem(tile_at - step + n_tiles, n_tiles)
            own = own + rs_buf[layer, other].astype(jnp.float32)
        pieces = []
        for at in range(own_heads):
            low, high = at * head_dim, (at + 1) * head_dim
            fine = cols + own_heads + at
            total = own[:, cols + at : cols + at + 1] + own[:, fine : fine + 1]
            piece = (own[:, low:high] / total).astype(jnp.bfloat16)
            attz_buf[layer, pl.ds(tile_at * tile_rows, tile_rows), low:high] = piece
            if layer + 1 < layers:
                att_buf[layer, member, :, low:high] = piece

    def spread_tiles(layer):
        mine = attz_buf.at[layer, pl.ds(tile_at * tile_rows, tile_rows)]
        copies = []
        for step in range(1, n_tiles):
            copies.append(
                remote(
                    mine,
                    mine,
                    attz_send.at[layer, step],
                    attz_recv.at[layer, step],
                    tile_peer(step),
                )
            )
            copies[-1].start()
        return copies

    def spread_members(layer):
        copies = []
        for step in range(1, members):
            other = lax.rem(member + step, members)
            copies.append(
                remote(
                    attz_buf.at[layer, pl.ds(other * own_rows, own_rows)],
                    fin_buf.at[layer, member],
                    fin_send.at[layer, step],
                    fin_recv.at[layer, step],
                    member_peer(step),
                )
            )
            copies[-1].start()
        return copies

    def project_out(layer, start, own_piece):
        total = start
        total = total + jnp.dot(
            own_piece, wout_buf[layer, member], preferred_element_type=jnp.float32
        )
        return total

    base = q_buf[pl.ds(tile_at * tile_rows, tile_rows)].astype(jnp.float32)
    final = q_buf[pl.ds(member * own_rows, own_rows)].astype(jnp.float32)
    pending = []
    for layer in range(layers):
        copies = attend(layer)
        if layer == 0:
            finish_item(1)
            for slot in range(slots):
                kv_copy(slot).wait_send()
        for hop in range(1, n_heads):
            if layer + 1 < layers:
                shares[2 + layer, hop].wait()
                start_relay(2 + layer, hop)
        if layer > 0:
            finish_item(1 + layer)
            own_w[layer].wait()
        merge(layer, copies)
        if layer + 1 < layers:
            mine = att_buf.at[layer, member]
            spread = []
            for step in range(1, members):
                spread.append(
                    remote(
                        mine,
                        mine,
                        att_send.at[layer, step],
                        att_recv.at[layer, step],
                        member_peer(step),
                    )
                )
                spread[-1].start()
            over_tiles = spread_tiles(layer)
            base = base + jnp.dot(
                att_buf[layer, member], wout_buf[layer, member], preferred_element_type=jnp.float32
            )
            for step in range(1, members):
                spread[step - 1].wait()
                other = lax.rem(member - step + members, members)
                base = base + jnp.dot(
                    att_buf[layer, other],
                    wout_buf[layer, other],
                    preferred_element_type=jnp.float32,
                )
            rows = pl.ds(tile_at * tile_rows, tile_rows)
            query_buf[layer + 1, rows] = to_query(base, layer + 1)
            gather = []
            for step in range(1, n_tiles):
                mine = query_buf.at[layer + 1, rows]
                gather.append(
                    remote(
                        mine,
                        mine,
                        qry_send.at[layer, step],
                        qry_recv.at[layer, step],
                        tile_peer(step),
                    )
                )
                gather[-1].start()
            for copy in over_tiles:
                copy.wait()
            pending.append(spread_members(layer))
            for copy in gather:
                copy.wait()
        else:
            over_tiles = spread_tiles(layer)
            for old, copies in enumerate(pending):
                own_piece = attz_buf[old, pl.ds(member * own_rows, own_rows)]
                final = project_out(old, final, own_piece)
                for step in range(1, members):
                    copies[step - 1].wait()
                    other = lax.rem(member - step + members, members)
                    final = final + jnp.dot(
                        fin_buf[old, other],
                        wout_buf[old, other],
                        preferred_element_type=jnp.float32,
                    )
            for copy in over_tiles:
                copy.wait()
            last = spread_members(layer)
            own_piece = attz_buf[layer, pl.ds(member * own_rows, own_rows)]
            final = project_out(layer, final, own_piece)
            for step in range(1, members):
                last[step - 1].wait()
                other = lax.rem(member - step + members, members)
                final = final + jnp.dot(
                    fin_buf[layer, other],
                    wout_buf[layer, other],
                    preferred_element_type=jnp.float32,
                )
            out_ref[...] = final


def fused_body(
    mesh, features, counts, tile_mask, queries, norm_gain, head_scale, w_query, w_kv, w_out
):
    n_tiles, n_heads, n_kv = (mesh.shape[name] for name in ("tiles", "heads", "kv"))
    members = n_heads * n_kv
    slots, block = tile_mask.shape
    own_rows, dq = queries.shape
    n_queries = own_rows * members
    tile_rows = n_queries // n_tiles
    layers, feat, _, side_cols = w_kv.shape
    cols = w_query.shape[2]
    own_heads = head_scale.shape[0] // n_kv
    head_dim = cols // own_heads
    width = -(-(cols + 2 * own_heads) // 128) * 128
    bf16, f32 = jnp.bfloat16, jnp.float32
    dma = pltpu.SemaphoreType.DMA
    any_spec = pl.BlockSpec(memory_space=pl.ANY)
    smem = pl.BlockSpec(memory_space=pltpu.SMEM)
    vmem = pl.BlockSpec(memory_space=pltpu.VMEM)
    return pl.pallas_call(
        functools.partial(fused_kernel, n_tiles, n_heads, n_kv),
        out_shape=jax.ShapeDtypeStruct((own_rows, dq), f32),
        in_specs=[smem, smem, vmem, vmem] + [any_spec] * 5,
        out_specs=vmem,
        scratch_shapes=[
            pltpu.VMEM((slots, block, feat), bf16),
            pltpu.VMEM((feat, layers * side_cols), bf16),
            pltpu.VMEM((layers, dq, cols), bf16),
            pltpu.VMEM((layers, members, cols, dq), bf16),
            pltpu.VMEM((n_queries, dq), bf16),
            pltpu.VMEM((slots, 2, layers, block, cols), bf16),
            pltpu.VMEM((slots, layers, block, cols), bf16),
            pltpu.VMEM((slots, block), f32),
            pltpu.VMEM((layers, n_queries, cols), bf16),
            pltpu.VMEM((own_heads, n_queries, head_dim), f32),
            pltpu.VMEM((own_heads, n_queries, 128), f32),
            pltpu.VMEM((layers, n_queries, width), bf16),
            pltpu.VMEM((layers, n_tiles, tile_rows, width), bf16),
            pltpu.VMEM((layers, members, tile_rows, cols), bf16),
            pltpu.VMEM((layers, n_queries, cols), bf16),
            pltpu.VMEM((layers, members, own_rows, cols), bf16),
            dma((layers + 1,)),
            dma((slots,)),
            dma((layers + 1,)),
            dma((layers + 1, n_heads)),
            dma((layers + 1, n_heads)),
            dma((layers + 1, n_heads)),
            dma((layers + 1, n_heads)),
            dma((slots,)),
            dma((slots,)),
            dma((layers, n_tiles)),
            dma((layers, n_tiles)),
            dma((layers, members)),
            dma((layers, members)),
            dma((layers, n_tiles)),
            dma((layers, n_tiles)),
            dma((layers, n_tiles)),
            dma((layers, n_tiles)),
            dma((layers, members)),
            dma((layers, members)),
        ],
        compiler_params=pltpu.CompilerParams(
            collective_id=0, has_side_effects=True, vmem_limit_bytes=56 * 1024 * 1024
        ),
    )(
        counts,
        head_scale,
        tile_mask,
        norm_gain,
        features,
        queries,
        w_query,
        w_kv.reshape(layers, feat, side_cols),
        w_out,
    )


def choose(mesh, *args):
    features, counts, tile_mask, queries, norm_gain, head_scale, w_query, w_kv, w_out = args
    n_tiles, n_heads, n_kv = (mesh.shape[name] for name in ("tiles", "heads", "kv"))
    n_queries = queries.shape[0] * n_heads * n_kv
    fits = (
        n_kv == 2
        and n_tiles > 1
        and n_heads > 1
        and head_scale.shape[0] % n_kv == 0
        and n_queries % (n_tiles * 16) == 0
        and queries.shape[0] % 16 == 0
        and tile_mask.shape[1] % 128 == 0
        and w_kv.shape[3] % 128 == 0
        and w_kv.shape[3] == n_kv * w_query.shape[2]
    )
    return fused_body(mesh, *args) if fits else body(*args)


def solution(mesh):
    return jax.shard_map(
        functools.partial(choose, mesh),
        mesh=mesh,
        in_specs=(
            P(("groups", "tiles"), None),
            P(("groups", "tiles")),
            P(("groups", "tiles"), None),
            P(("heads", "kv"), None),
            P(),
            P("heads"),
            P(None, None, ("heads", "kv")),
            P(None, None, "kv", "heads"),
            P(None, ("heads", "kv"), None),
        ),
        out_specs=P(("groups", "heads", "kv"), None),
        check_vma=False,
    )
```

```python
import functools
import math

import jax
import jax.numpy as jnp
from jax import lax
from jax.experimental import pallas as pl
from jax.experimental.pallas import tpu as pltpu
from jax.sharding import PartitionSpec as P

SOFT_CAP = 50.0
NORM_EPS = 1e-06


def normalize(hidden, gain_row):
    return (
        hidden * lax.rsqrt(jnp.mean(hidden * hidden, axis=-1, keepdims=True) + NORM_EPS) * gain_row
    )


def body(features, counts, tile_mask, queries, norm_gain, head_scale, w_query, w_kv, w_out):
    slot_count = tile_mask.shape[0]
    block_rows = tile_mask.shape[1]
    total_rows = slot_count * block_rows
    half_rows = total_rows // 2
    layer_count = w_kv.shape[0]
    head_cols = w_kv.shape[3]
    heads_local = head_scale.shape[0]
    head_dim = head_cols // heads_local
    kv_side = lax.axis_index("kv")
    kv_weights = w_kv[:, :, 0, :]
    slot_ids = jnp.arange(slot_count, dtype=jnp.int32)

    def add_block(slot_at, current):
        block_feats = lax.dynamic_slice_in_dim(features, slot_at * block_rows, block_rows, 0)
        result = jnp.einsum(
            "rf,lfc->lrc", block_feats, kv_weights, preferred_element_type=jnp.float32
        )
        return lax.dynamic_update_slice_in_dim(
            current, result.astype(jnp.bfloat16), slot_at * block_rows, 1
        )

    own_count = counts[0]
    projected = jnp.zeros((layer_count, total_rows, head_cols), jnp.bfloat16)
    projected = lax.fori_loop(jnp.int32(0), own_count, add_block, projected)
    live_mask = tile_mask * (slot_ids < own_count).astype(jnp.int32)[:, None]
    kv_local = lax.all_to_all(projected, "kv", split_axis=1, concat_axis=2, tiled=True)
    valid_tiles = lax.dynamic_slice_in_dim(
        live_mask.reshape(total_rows).astype(jnp.float32), kv_side * half_rows, half_rows, 0
    )
    states = queries.astype(jnp.float32)
    scale_vec = head_scale / math.sqrt(head_dim)
    for layer_at in range(layer_count):
        normed = lax.all_gather(
            normalize(states, norm_gain[layer_at]).astype(jnp.bfloat16),
            ("heads", "kv"),
            axis=0,
            tiled=True,
        )
        query_part = jnp.dot(normed, w_query[layer_at], preferred_element_type=jnp.float32).astype(
            jnp.bfloat16
        )
        query_cols = lax.all_gather(query_part, "kv", axis=1, tiled=True)
        n_queries = query_cols.shape[0]
        query_heads = query_cols.reshape(n_queries, heads_local, head_dim)
        key_heads = kv_local[layer_at, :, :head_cols].reshape(half_rows, heads_local, head_dim)
        value_heads = kv_local[layer_at, :, head_cols:].reshape(half_rows, heads_local, head_dim)
        scores = jnp.einsum(
            "qhd,khd->hqk", query_heads, key_heads, preferred_element_type=jnp.float32
        )
        scores = scores * scale_vec[:, None, None]
        capped = SOFT_CAP * jnp.tanh(scores / SOFT_CAP)
        weights_p = jnp.exp(capped) * valid_tiles[None, None, :]
        totals = jnp.sum(weights_p, axis=2)
        partial_value = jnp.einsum(
            "hqk,khd->qhd",
            weights_p.astype(jnp.bfloat16),
            value_heads,
            preferred_element_type=jnp.float32,
        )
        totals, partial_value = lax.psum((totals, partial_value), ("tiles", "kv"))
        attended = (
            (partial_value / jnp.transpose(totals)[:, :, None])
            .reshape(n_queries, head_cols)
            .astype(jnp.bfloat16)
        )
        own_cols = lax.dynamic_slice_in_dim(attended, kv_side * (head_cols // 2), head_cols // 2, 1)
        states = states + lax.psum_scatter(
            jnp.dot(own_cols, w_out[layer_at], preferred_element_type=jnp.float32),
            ("heads", "kv"),
            scatter_dimension=0,
            tiled=True,
        )
    return states


MESH = pl.DeviceIdType.MESH


def fused_kernel(
    n_tiles,
    n_heads,
    n_kv,
    counts_ref,
    scale_ref,
    mask_ref,
    gain_ref,
    features,
    queries,
    w_query,
    w_kv,
    w_out,
    out_ref,
    feat_buf,
    kvw_buf,
    wq_buf,
    wout_buf,
    q_buf,
    kv_buf,
    kv_out,
    valid_buf,
    query_buf,
    acc_buf,
    tot_buf,
    part_buf,
    rs_buf,
    att_buf,
    attz_buf,
    fin_buf,
    load_sem,
    feat_sem,
    own_sem,
    share_send,
    share_recv,
    relay_send,
    relay_recv,
    kv_send,
    kv_recv,
    rs_send,
    rs_recv,
    att_send,
    att_recv,
    qry_send,
    qry_recv,
    attz_send,
    attz_recv,
    fin_send,
    fin_recv,
):
    tile_at = lax.axis_index("tiles")
    head_at = lax.axis_index("heads")
    kv_at = lax.axis_index("kv")
    members = n_heads * n_kv
    member = head_at * n_kv + kv_at
    slots, block, _ = feat_buf.shape
    layers = wq_buf.shape[0]
    cols = wq_buf.shape[1]
    width = rs_buf.shape[3]
    own_heads = acc_buf.shape[0]
    head_dim = acc_buf.shape[2]
    n_queries, dq = q_buf.shape
    tile_rows = n_queries // n_tiles
    own_rows = n_queries // members
    side_cols = w_kv.shape[2]

    def tile_peer(step):
        return {"tiles": lax.rem(tile_at + step, n_tiles)}

    def member_peer(step):
        other = lax.rem(member + step, members)
        return {"heads": other // n_kv, "kv": lax.rem(other, n_kv)}

    def remote(src, dst, send, recv, where):
        return pltpu.make_async_remote_copy(
            src_ref=src,
            dst_ref=dst,
            send_sem=send,
            recv_sem=recv,
            device_id=where,
            device_id_type=MESH,
        )

    barrier = pltpu.get_barrier_semaphore()
    for step in range(1, n_tiles):
        pl.semaphore_signal(barrier, inc=1, device_id=tile_peer(step), device_id_type=MESH)
    for step in range(1, members):
        pl.semaphore_signal(barrier, inc=1, device_id=member_peer(step), device_id_type=MESH)

    loads = [
        pltpu.make_async_copy(
            w_kv.at[layer],
            kvw_buf.at[:, pl.ds(layer * side_cols, side_cols)],
            load_sem.at[layer],
        )
        for layer in range(layers)
    ]
    feat_loads = [
        pltpu.make_async_copy(
            features.at[pl.ds(slot * block, block)], feat_buf.at[slot], feat_sem.at[slot]
        )
        for slot in range(slots)
    ]
    wq_load = pltpu.make_async_copy(w_query, wq_buf, load_sem.at[layers])
    for copy in loads[:1] + feat_loads[:1] + loads[1:] + feat_loads[1:]:
        copy.start()
    wq_load.start()
    own_q = pltpu.make_async_copy(
        queries, q_buf.at[pl.ds(member * own_rows, own_rows)], own_sem.at[0]
    )
    own_w = [
        pltpu.make_async_copy(w_out.at[layer], wout_buf.at[layer, member], own_sem.at[1 + layer])
        for layer in range(layers)
    ]
    own_q.start()
    for copy in own_w:
        copy.start()

    def item_at(item, owner):
        if item == 0:
            return q_buf.at[pl.ds(owner * own_rows, own_rows)]
        return wout_buf.at[item - 1, owner]

    def kv_copy(slot):
        return remote(
            kv_out.at[slot],
            kv_buf.at[slot, kv_at],
            kv_send.at[slot],
            kv_recv.at[slot],
            {"kv": lax.rem(kv_at + 1, n_kv)},
        )

    for copy in loads:
        copy.wait()

    def project(send, slot, carry):
        pltpu.make_async_copy(
            features.at[pl.ds(0, block)], feat_buf.at[slot], feat_sem.at[slot]
        ).wait()
        rows = jnp.dot(feat_buf[slot], kvw_buf[...], preferred_element_type=jnp.float32)
        for layer in range(layers):
            at = layer * side_cols
            low = rows[:, at : at + cols]
            high = rows[:, at + cols : at + 2 * cols]
            first = kv_at == 0
            kv_buf[slot, kv_at, layer] = jnp.where(first, low, high).astype(jnp.bfloat16)
            kv_out[slot, layer] = jnp.where(first, high, low).astype(jnp.bfloat16)
        if send:
            kv_copy(slot).start()
        return carry

    early = slots // 3
    middle = slots - slots // 3
    lax.fori_loop(0, early, functools.partial(project, False), 0)
    pl.semaphore_wait(barrier, n_tiles - 1 + members - 1)

    sources = [queries] + [w_out.at[layer] for layer in range(layers)]
    items = range(len(sources))
    shares = {}
    for item in items:
        for hop in range(1, n_heads):
            shares[item, hop] = remote(
                sources[item],
                item_at(item, member),
                share_send.at[item, hop],
                share_recv.at[item, hop],
                {"heads": lax.rem(head_at + hop, n_heads)},
            )
            shares[item, hop].start()
    relays = {}

    def start_relay(item, hop):
        owner = lax.rem(head_at - hop + n_heads, n_heads) * n_kv + kv_at
        src = sources[item] if hop == 0 else item_at(item, owner)
        relays[item, hop] = remote(
            src,
            item_at(item, owner),
            relay_send.at[item, hop],
            relay_recv.at[item, hop],
            {"kv": lax.rem(kv_at + 1, n_kv)},
        )
        relays[item, hop].start()

    def finish_item(item):
        for hop in range(n_heads):
            relays[item, hop].wait()

    for item in items:
        start_relay(item, 0)

    live = lax.broadcasted_iota(jnp.int32, mask_ref.shape, 0) < counts_ref[0]
    valid_buf[...] = jnp.where(live, mask_ref[...], 0).astype(jnp.float32)

    for slot in range(early):
        kv_copy(slot).start()
    lax.fori_loop(early, middle, functools.partial(project, True), 0)
    own_q.wait()
    for hop in range(1, n_heads):
        shares[0, hop].wait()
        start_relay(0, hop)
    lax.fori_loop(middle, slots, functools.partial(project, True), 0)
    finish_item(0)
    wq_load.wait()

    def to_query(states, layer):
        normed = normalize(states, gain_ref[pl.ds(layer, 1)]).astype(jnp.bfloat16)
        return lax.dot_general(
            normed,
            wq_buf[layer],
            (((1,), (1,)), ((), ())),
            preferred_element_type=jnp.float32,
        ).astype(jnp.bfloat16)

    query_buf[0] = to_query(q_buf[...].astype(jnp.float32), 0)
    own_w[0].wait()
    for hop in range(1, n_heads):
        shares[1, hop].wait()
        start_relay(1, hop)

    def attend(layer):
        acc_buf[...] = jnp.zeros_like(acc_buf)
        tot_buf[...] = jnp.zeros_like(tot_buf)
        lanes = tot_buf.shape[2]

        def add_block(slot, carry):
            if layer == 0:
                kv_copy(slot).wait_recv()
            valid_row = valid_buf[pl.ds(slot, 1)]
            for at in range(own_heads):
                low, high = at * head_dim, (at + 1) * head_dim
                scale = scale_ref[kv_at * own_heads + at] * (
                    1.0 / (math.sqrt(head_dim) * SOFT_CAP)
                )
                scores = lax.dot_general(
                    query_buf[layer, :, low:high],
                    kv_buf[slot, 0, layer, :, low:high],
                    (((1,), (1,)), ((), ())),
                    preferred_element_type=jnp.float32,
                )
                weights = jnp.exp(SOFT_CAP * jnp.tanh(scores * scale)) * valid_row
                total = weights[:, :lanes]
                for part in range(1, block // lanes):
                    total = total + weights[:, part * lanes : (part + 1) * lanes]
                tot_buf[at] += total
                acc_buf[at] += jnp.dot(
                    weights.astype(jnp.bfloat16),
                    kv_buf[slot, 1, layer, :, low:high],
                    preferred_element_type=jnp.float32,
                )
            return carry

        lax.fori_loop(0, slots, add_block, 0)
        tail_width = width - cols
        lane = lax.broadcasted_iota(jnp.int32, (n_queries, tail_width), 1)
        tail = jnp.zeros((n_queries, tail_width), jnp.float32)
        for at in range(own_heads):
            part_buf[layer, :, at * head_dim : (at + 1) * head_dim] = acc_buf[at].astype(
                jnp.bfloat16
            )
            total = jnp.sum(tot_buf[at], axis=1, keepdims=True)
            coarse = total.astype(jnp.bfloat16).astype(jnp.float32)
            tail = jnp.where(lane == at, coarse, tail)
            tail = jnp.where(lane == own_heads + at, total - coarse, tail)
        part_buf[layer, :, cols:width] = tail.astype(jnp.bfloat16)
        copies = []
        for step in range(1, n_tiles):
            other = lax.rem(tile_at + step, n_tiles)
            copies.append(
                remote(
                    part_buf.at[layer, pl.ds(other * tile_rows, tile_rows)],
                    rs_buf.at[layer, tile_at],
                    rs_send.at[layer, step],
                    rs_recv.at[layer, step],
                    tile_peer(step),
                )
            )
            copies[-1].start()
        return copies

    def merge(layer, copies):
        own = part_buf[layer, pl.ds(tile_at * tile_rows, tile_rows)].astype(jnp.float32)
        for step in range(1, n_tiles):
            copies[step - 1].wait()
            other = lax.rem(tile_at - step + n_tiles, n_tiles)
            own = own + rs_buf[layer, other].astype(jnp.float32)
        pieces = []
        for at in range(own_heads):
            low, high = at * head_dim, (at + 1) * head_dim
            fine = cols + own_heads + at
            total = own[:, cols + at : cols + at + 1] + own[:, fine : fine + 1]
            piece = (own[:, low:high] / total).astype(jnp.bfloat16)
            attz_buf[layer, pl.ds(tile_at * tile_rows, tile_rows), low:high] = piece
            if layer + 1 < layers:
                att_buf[layer, member, :, low:high] = piece

    def spread_tiles(layer):
        mine = attz_buf.at[layer, pl.ds(tile_at * tile_rows, tile_rows)]
        copies = []
        for step in range(1, n_tiles):
            copies.append(
                remote(
                    mine,
                    mine,
                    attz_send.at[layer, step],
                    attz_recv.at[layer, step],
                    tile_peer(step),
                )
            )
            copies[-1].start()
        return copies

    def spread_members(layer):
        copies = []
        for step in range(1, members):
            other = lax.rem(member + step, members)
            copies.append(
                remote(
                    attz_buf.at[layer, pl.ds(other * own_rows, own_rows)],
                    fin_buf.at[layer, member],
                    fin_send.at[layer, step],
                    fin_recv.at[layer, step],
                    member_peer(step),
                )
            )
            copies[-1].start()
        return copies

    def project_out(layer, start, own_piece):
        total = start
        total = total + jnp.dot(
            own_piece, wout_buf[layer, member], preferred_element_type=jnp.float32
        )
        return total

    base = q_buf[pl.ds(tile_at * tile_rows, tile_rows)].astype(jnp.float32)
    final = q_buf[pl.ds(member * own_rows, own_rows)].astype(jnp.float32)
    pending = []
    for layer in range(layers):
        copies = attend(layer)
        if layer == 0:
            finish_item(1)
            for slot in range(slots):
                kv_copy(slot).wait_send()
        for hop in range(1, n_heads):
            if layer + 1 < layers:
                shares[2 + layer, hop].wait()
                start_relay(2 + layer, hop)
        if layer > 0:
            finish_item(1 + layer)
            own_w[layer].wait()
        merge(layer, copies)
        if layer + 1 < layers:
            mine = att_buf.at[layer, member]
            spread = []
            for step in range(1, members):
                spread.append(
                    remote(
                        mine,
                        mine,
                        att_send.at[layer, step],
                        att_recv.at[layer, step],
                        member_peer(step),
                    )
                )
                spread[-1].start()
            over_tiles = spread_tiles(layer)
            base = base + jnp.dot(
                att_buf[layer, member], wout_buf[layer, member], preferred_element_type=jnp.float32
            )
            for step in range(1, members):
                spread[step - 1].wait()
                other = lax.rem(member - step + members, members)
                base = base + jnp.dot(
                    att_buf[layer, other],
                    wout_buf[layer, other],
                    preferred_element_type=jnp.float32,
                )
            rows = pl.ds(tile_at * tile_rows, tile_rows)
            query_buf[layer + 1, rows] = to_query(base, layer + 1)
            gather = []
            for step in range(1, n_tiles):
                mine = query_buf.at[layer + 1, rows]
                gather.append(
                    remote(
                        mine,
                        mine,
                        qry_send.at[layer, step],
                        qry_recv.at[layer, step],
                        tile_peer(step),
                    )
                )
                gather[-1].start()
            for copy in over_tiles:
                copy.wait()
            pending.append(spread_members(layer))
            for copy in gather:
                copy.wait()
        else:
            over_tiles = spread_tiles(layer)
            for old, copies in enumerate(pending):
                own_piece = attz_buf[old, pl.ds(member * own_rows, own_rows)]
                final = project_out(old, final, own_piece)
                for step in range(1, members):
                    copies[step - 1].wait()
                    other = lax.rem(member - step + members, members)
                    final = final + jnp.dot(
                        fin_buf[old, other],
                        wout_buf[old, other],
                        preferred_element_type=jnp.float32,
                    )
            for copy in over_tiles:
                copy.wait()
            last = spread_members(layer)
            own_piece = attz_buf[layer, pl.ds(member * own_rows, own_rows)]
            final = project_out(layer, final, own_piece)
            for step in range(1, members):
                last[step - 1].wait()
                other = lax.rem(member - step + members, members)
                final = final + jnp.dot(
                    fin_buf[layer, other],
                    wout_buf[layer, other],
                    preferred_element_type=jnp.float32,
                )
            out_ref[...] = final


def fused_body(
    mesh, features, counts, tile_mask, queries, norm_gain, head_scale, w_query, w_kv, w_out
):
    n_tiles, n_heads, n_kv = (mesh.shape[name] for name in ("tiles", "heads", "kv"))
    members = n_heads * n_kv
    slots, block = tile_mask.shape
    own_rows, dq = queries.shape
    n_queries = own_rows * members
    tile_rows = n_queries // n_tiles
    layers, feat, _, side_cols = w_kv.shape
    cols = w_query.shape[2]
    own_heads = head_scale.shape[0] // n_kv
    head_dim = cols // own_heads
    width = -(-(cols + 2 * own_heads) // 128) * 128
    bf16, f32 = jnp.bfloat16, jnp.float32
    dma = pltpu.SemaphoreType.DMA
    any_spec = pl.BlockSpec(memory_space=pl.ANY)
    smem = pl.BlockSpec(memory_space=pltpu.SMEM)
    vmem = pl.BlockSpec(memory_space=pltpu.VMEM)
    return pl.pallas_call(
        functools.partial(fused_kernel, n_tiles, n_heads, n_kv),
        out_shape=jax.ShapeDtypeStruct((own_rows, dq), f32),
        in_specs=[smem, smem, vmem, vmem] + [any_spec] * 5,
        out_specs=vmem,
        scratch_shapes=[
            pltpu.VMEM((slots, block, feat), bf16),
            pltpu.VMEM((feat, layers * side_cols), bf16),
            pltpu.VMEM((layers, cols, dq), bf16),
            pltpu.VMEM((layers, members, cols, dq), bf16),
            pltpu.VMEM((n_queries, dq), bf16),
            pltpu.VMEM((slots, 2, layers, block, cols), bf16),
            pltpu.VMEM((slots, layers, block, cols), bf16),
            pltpu.VMEM((slots, block), f32),
            pltpu.VMEM((layers, n_queries, cols), bf16),
            pltpu.VMEM((own_heads, n_queries, head_dim), f32),
            pltpu.VMEM((own_heads, n_queries, 128), f32),
            pltpu.VMEM((layers, n_queries, width), bf16),
            pltpu.VMEM((layers, n_tiles, tile_rows, width), bf16),
            pltpu.VMEM((layers, members, tile_rows, cols), bf16),
            pltpu.VMEM((layers, n_queries, cols), bf16),
            pltpu.VMEM((layers, members, own_rows, cols), bf16),
            dma((layers + 1,)),
            dma((slots,)),
            dma((layers + 1,)),
            dma((layers + 1, n_heads)),
            dma((layers + 1, n_heads)),
            dma((layers + 1, n_heads)),
            dma((layers + 1, n_heads)),
            dma((slots,)),
            dma((slots,)),
            dma((layers, n_tiles)),
            dma((layers, n_tiles)),
            dma((layers, members)),
            dma((layers, members)),
            dma((layers, n_tiles)),
            dma((layers, n_tiles)),
            dma((layers, n_tiles)),
            dma((layers, n_tiles)),
            dma((layers, members)),
            dma((layers, members)),
        ],
        compiler_params=pltpu.CompilerParams(
            collective_id=0, has_side_effects=True, vmem_limit_bytes=56 * 1024 * 1024
        ),
    )(
        counts,
        head_scale,
        tile_mask,
        norm_gain,
        features,
        queries,
        jnp.swapaxes(w_query, 1, 2),
        w_kv.reshape(layers, feat, side_cols),
        w_out,
    )


def choose(mesh, *args):
    features, counts, tile_mask, queries, norm_gain, head_scale, w_query, w_kv, w_out = args
    n_tiles, n_heads, n_kv = (mesh.shape[name] for name in ("tiles", "heads", "kv"))
    n_queries = queries.shape[0] * n_heads * n_kv
    fits = (
        n_kv == 2
        and n_tiles > 1
        and n_heads > 1
        and head_scale.shape[0] % n_kv == 0
        and n_queries % (n_tiles * 16) == 0
        and queries.shape[0] % 16 == 0
        and tile_mask.shape[1] % 128 == 0
        and w_kv.shape[3] % 128 == 0
        and w_kv.shape[3] == n_kv * w_query.shape[2]
    )
    return fused_body(mesh, *args) if fits else body(*args)


def solution(mesh):
    return jax.shard_map(
        functools.partial(choose, mesh),
        mesh=mesh,
        in_specs=(
            P(("groups", "tiles"), None),
            P(("groups", "tiles")),
            P(("groups", "tiles"), None),
            P(("heads", "kv"), None),
            P(),
            P("heads"),
            P(None, None, ("heads", "kv")),
            P(None, None, "kv", "heads"),
            P(None, ("heads", "kv"), None),
        ),
        out_specs=P(("groups", "heads", "kv"), None),
        check_vma=False,
    )
```

```python
import functools
import math

import jax
import jax.numpy as jnp
from jax import lax
from jax.experimental import pallas as pl
from jax.experimental.pallas import tpu as pltpu
from jax.sharding import PartitionSpec as P

SOFT_CAP = 50.0
NORM_EPS = 1e-06


def normalize(hidden, gain_row):
    return (
        hidden * lax.rsqrt(jnp.mean(hidden * hidden, axis=-1, keepdims=True) + NORM_EPS) * gain_row
    )


def body(features, counts, tile_mask, queries, norm_gain, head_scale, w_query, w_kv, w_out):
    slot_count = tile_mask.shape[0]
    block_rows = tile_mask.shape[1]
    total_rows = slot_count * block_rows
    half_rows = total_rows // 2
    layer_count = w_kv.shape[0]
    head_cols = w_kv.shape[3]
    heads_local = head_scale.shape[0]
    head_dim = head_cols // heads_local
    kv_side = lax.axis_index("kv")
    kv_weights = w_kv[:, :, 0, :]
    slot_ids = jnp.arange(slot_count, dtype=jnp.int32)

    def add_block(slot_at, current):
        block_feats = lax.dynamic_slice_in_dim(features, slot_at * block_rows, block_rows, 0)
        result = jnp.einsum(
            "rf,lfc->lrc", block_feats, kv_weights, preferred_element_type=jnp.float32
        )
        return lax.dynamic_update_slice_in_dim(
            current, result.astype(jnp.bfloat16), slot_at * block_rows, 1
        )

    own_count = counts[0]
    projected = jnp.zeros((layer_count, total_rows, head_cols), jnp.bfloat16)
    projected = lax.fori_loop(jnp.int32(0), own_count, add_block, projected)
    live_mask = tile_mask * (slot_ids < own_count).astype(jnp.int32)[:, None]
    kv_local = lax.all_to_all(projected, "kv", split_axis=1, concat_axis=2, tiled=True)
    valid_tiles = lax.dynamic_slice_in_dim(
        live_mask.reshape(total_rows).astype(jnp.float32), kv_side * half_rows, half_rows, 0
    )
    states = queries.astype(jnp.float32)
    scale_vec = head_scale / math.sqrt(head_dim)
    for layer_at in range(layer_count):
        normed = lax.all_gather(
            normalize(states, norm_gain[layer_at]).astype(jnp.bfloat16),
            ("heads", "kv"),
            axis=0,
            tiled=True,
        )
        query_part = jnp.dot(normed, w_query[layer_at], preferred_element_type=jnp.float32).astype(
            jnp.bfloat16
        )
        query_cols = lax.all_gather(query_part, "kv", axis=1, tiled=True)
        n_queries = query_cols.shape[0]
        query_heads = query_cols.reshape(n_queries, heads_local, head_dim)
        key_heads = kv_local[layer_at, :, :head_cols].reshape(half_rows, heads_local, head_dim)
        value_heads = kv_local[layer_at, :, head_cols:].reshape(half_rows, heads_local, head_dim)
        scores = jnp.einsum(
            "qhd,khd->hqk", query_heads, key_heads, preferred_element_type=jnp.float32
        )
        scores = scores * scale_vec[:, None, None]
        capped = SOFT_CAP * jnp.tanh(scores / SOFT_CAP)
        weights_p = jnp.exp(capped) * valid_tiles[None, None, :]
        totals = jnp.sum(weights_p, axis=2)
        partial_value = jnp.einsum(
            "hqk,khd->qhd",
            weights_p.astype(jnp.bfloat16),
            value_heads,
            preferred_element_type=jnp.float32,
        )
        totals, partial_value = lax.psum((totals, partial_value), ("tiles", "kv"))
        attended = (
            (partial_value / jnp.transpose(totals)[:, :, None])
            .reshape(n_queries, head_cols)
            .astype(jnp.bfloat16)
        )
        own_cols = lax.dynamic_slice_in_dim(attended, kv_side * (head_cols // 2), head_cols // 2, 1)
        states = states + lax.psum_scatter(
            jnp.dot(own_cols, w_out[layer_at], preferred_element_type=jnp.float32),
            ("heads", "kv"),
            scatter_dimension=0,
            tiled=True,
        )
    return states


LOG2_E = math.log2(math.e)
MESH = pl.DeviceIdType.MESH


def fused_kernel(
    n_tiles,
    n_heads,
    n_kv,
    counts_ref,
    scale_ref,
    mask_ref,
    gain_ref,
    features,
    queries,
    w_query,
    w_kv,
    w_out,
    out_ref,
    feat_buf,
    kvw_buf,
    wq_buf,
    wout_buf,
    q_buf,
    kv_buf,
    kv_out,
    valid_buf,
    query_buf,
    acc_buf,
    tot_buf,
    part_buf,
    rs_buf,
    att_buf,
    attz_buf,
    fin_buf,
    load_sem,
    feat_sem,
    own_sem,
    share_send,
    share_recv,
    relay_send,
    relay_recv,
    kv_send,
    kv_recv,
    rs_send,
    rs_recv,
    att_send,
    att_recv,
    qry_send,
    qry_recv,
    attz_send,
    attz_recv,
    fin_send,
    fin_recv,
):
    tile_at = lax.axis_index("tiles")
    head_at = lax.axis_index("heads")
    kv_at = lax.axis_index("kv")
    members = n_heads * n_kv
    member = head_at * n_kv + kv_at
    slots, block, _ = feat_buf.shape
    layers = wq_buf.shape[0]
    cols = wq_buf.shape[1]
    width = rs_buf.shape[3]
    own_heads = acc_buf.shape[0]
    head_dim = acc_buf.shape[2]
    n_queries, dq = q_buf.shape
    tile_rows = n_queries // n_tiles
    own_rows = n_queries // members
    side_cols = w_kv.shape[2]

    def tile_peer(step):
        return {"tiles": lax.rem(tile_at + step, n_tiles)}

    def member_peer(step):
        other = lax.rem(member + step, members)
        return {"heads": other // n_kv, "kv": lax.rem(other, n_kv)}

    def remote(src, dst, send, recv, where):
        return pltpu.make_async_remote_copy(
            src_ref=src,
            dst_ref=dst,
            send_sem=send,
            recv_sem=recv,
            device_id=where,
            device_id_type=MESH,
        )

    barrier = pltpu.get_barrier_semaphore()
    for step in range(1, n_tiles):
        pl.semaphore_signal(barrier, inc=1, device_id=tile_peer(step), device_id_type=MESH)
    for step in range(1, members):
        pl.semaphore_signal(barrier, inc=1, device_id=member_peer(step), device_id_type=MESH)

    loads = [
        pltpu.make_async_copy(
            w_kv.at[layer],
            kvw_buf.at[:, pl.ds(layer * side_cols, side_cols)],
            load_sem.at[layer],
        )
        for layer in range(layers)
    ]
    feat_loads = [
        pltpu.make_async_copy(
            features.at[pl.ds(slot * block, block)], feat_buf.at[slot], feat_sem.at[slot]
        )
        for slot in range(slots)
    ]
    wq_load = pltpu.make_async_copy(w_query, wq_buf, load_sem.at[layers])
    for copy in loads[:1] + feat_loads[:1] + loads[1:] + feat_loads[1:]:
        copy.start()
    wq_load.start()
    own_q = pltpu.make_async_copy(
        queries, q_buf.at[pl.ds(member * own_rows, own_rows)], own_sem.at[0]
    )
    own_w = [
        pltpu.make_async_copy(w_out.at[layer], wout_buf.at[layer, member], own_sem.at[1 + layer])
        for layer in range(layers)
    ]
    own_q.start()
    for copy in own_w:
        copy.start()

    def item_at(item, owner):
        if item == 0:
            return q_buf.at[pl.ds(owner * own_rows, own_rows)]
        return wout_buf.at[item - 1, owner]

    def kv_copy(slot):
        return remote(
            kv_out.at[slot],
            kv_buf.at[slot, kv_at],
            kv_send.at[slot],
            kv_recv.at[slot],
            {"kv": lax.rem(kv_at + 1, n_kv)},
        )

    def project(slot, carry):
        pltpu.make_async_copy(
            features.at[pl.ds(0, block)], feat_buf.at[slot], feat_sem.at[slot]
        ).wait()
        rows = jnp.dot(feat_buf[slot], kvw_buf[...], preferred_element_type=jnp.float32)
        for layer in range(layers):
            at = layer * side_cols
            low = rows[:, at : at + cols]
            high = rows[:, at + cols : at + 2 * cols]
            first = kv_at == 0
            kv_buf[slot, kv_at, layer] = jnp.where(first, low, high).astype(jnp.bfloat16)
            kv_out[slot, layer] = jnp.where(first, high, low).astype(jnp.bfloat16)
        kv_copy(slot).start()
        return carry

    middle = slots - slots // 3
    pl.semaphore_wait(barrier, n_tiles - 1 + members - 1)

    sources = [queries] + [w_out.at[layer] for layer in range(layers)]
    items = range(len(sources))
    shares = {}
    for item in items:
        for hop in range(1, n_heads):
            shares[item, hop] = remote(
                sources[item],
                item_at(item, member),
                share_send.at[item, hop],
                share_recv.at[item, hop],
                {"heads": lax.rem(head_at + hop, n_heads)},
            )
            shares[item, hop].start()
    relays = {}

    def start_relay(item, hop):
        owner = lax.rem(head_at - hop + n_heads, n_heads) * n_kv + kv_at
        src = sources[item] if hop == 0 else item_at(item, owner)
        relays[item, hop] = remote(
            src,
            item_at(item, owner),
            relay_send.at[item, hop],
            relay_recv.at[item, hop],
            {"kv": lax.rem(kv_at + 1, n_kv)},
        )
        relays[item, hop].start()

    def finish_item(item):
        for hop in range(n_heads):
            relays[item, hop].wait()

    for item in items:
        start_relay(item, 0)

    live = lax.broadcasted_iota(jnp.int32, mask_ref.shape, 0) < counts_ref[0]
    valid_buf[...] = jnp.where(live, mask_ref[...], 0).astype(jnp.float32)

    for copy in loads:
        copy.wait()
    lax.fori_loop(0, middle, project, 0, unroll=2)
    own_q.wait()
    for hop in range(1, n_heads):
        shares[0, hop].wait()
        start_relay(0, hop)
    lax.fori_loop(middle, slots, project, 0, unroll=2)
    finish_item(0)
    wq_load.wait()

    def to_query(states, layer):
        normed = normalize(states, gain_ref[pl.ds(layer, 1)]).astype(jnp.bfloat16)
        return lax.dot_general(
            normed,
            wq_buf[layer],
            (((1,), (1,)), ((), ())),
            preferred_element_type=jnp.float32,
        ).astype(jnp.bfloat16)

    query_buf[0] = to_query(q_buf[...].astype(jnp.float32), 0)
    own_w[0].wait()
    for hop in range(1, n_heads):
        shares[1, hop].wait()
        start_relay(1, hop)

    def attend(layer):
        acc_buf[...] = jnp.zeros_like(acc_buf)
        tot_buf[...] = jnp.zeros_like(tot_buf)
        lanes = tot_buf.shape[2]

        def add_block(slot, carry):
            if layer == 0:
                kv_copy(slot).wait_recv()
            valid_row = valid_buf[pl.ds(slot, 1)]
            for at in range(own_heads):
                low, high = at * head_dim, (at + 1) * head_dim
                scale = scale_ref[kv_at * own_heads + at] * (
                    1.0 / (math.sqrt(head_dim) * SOFT_CAP)
                )
                scores = lax.dot_general(
                    query_buf[layer, :, low:high],
                    kv_buf[slot, 0, layer, :, low:high],
                    (((1,), (1,)), ((), ())),
                    preferred_element_type=jnp.float32,
                )
                weights = jnp.exp2((SOFT_CAP * LOG2_E) * jnp.tanh(scores * scale)) * valid_row
                total = weights[:, :lanes]
                for part in range(1, block // lanes):
                    total = total + weights[:, part * lanes : (part + 1) * lanes]
                tot_buf[at] += total
                acc_buf[at] += jnp.dot(
                    weights.astype(jnp.bfloat16),
                    kv_buf[slot, 1, layer, :, low:high],
                    preferred_element_type=jnp.float32,
                )
            return carry

        lax.fori_loop(0, slots, add_block, 0, unroll=True)
        tail_width = width - cols
        lane = lax.broadcasted_iota(jnp.int32, (n_queries, tail_width), 1)
        tail = jnp.zeros((n_queries, tail_width), jnp.float32)
        for at in range(own_heads):
            part_buf[layer, :, at * head_dim : (at + 1) * head_dim] = acc_buf[at].astype(
                jnp.bfloat16
            )
            total = jnp.sum(tot_buf[at], axis=1, keepdims=True)
            coarse = total.astype(jnp.bfloat16).astype(jnp.float32)
            tail = jnp.where(lane == at, coarse, tail)
            tail = jnp.where(lane == own_heads + at, total - coarse, tail)
        part_buf[layer, :, cols:width] = tail.astype(jnp.bfloat16)
        copies = []
        for step in range(1, n_tiles):
            other = lax.rem(tile_at + step, n_tiles)
            copies.append(
                remote(
                    part_buf.at[layer, pl.ds(other * tile_rows, tile_rows)],
                    rs_buf.at[layer, tile_at],
                    rs_send.at[layer, step],
                    rs_recv.at[layer, step],
                    tile_peer(step),
                )
            )
            copies[-1].start()
        return copies

    def merge(layer, copies):
        own = part_buf[layer, pl.ds(tile_at * tile_rows, tile_rows)].astype(jnp.float32)
        for step in range(1, n_tiles):
            copies[step - 1].wait()
            other = lax.rem(tile_at - step + n_tiles, n_tiles)
            own = own + rs_buf[layer, other].astype(jnp.float32)
        pieces = []
        for at in range(own_heads):
            low, high = at * head_dim, (at + 1) * head_dim
            fine = cols + own_heads + at
            total = own[:, cols + at : cols + at + 1] + own[:, fine : fine + 1]
            piece = (own[:, low:high] / total).astype(jnp.bfloat16)
            attz_buf[layer, pl.ds(tile_at * tile_rows, tile_rows), low:high] = piece
            if layer + 1 < layers:
                att_buf[layer, member, :, low:high] = piece

    def spread_tiles(layer):
        mine = attz_buf.at[layer, pl.ds(tile_at * tile_rows, tile_rows)]
        copies = []
        for step in range(1, n_tiles):
            copies.append(
                remote(
                    mine,
                    mine,
                    attz_send.at[layer, step],
                    attz_recv.at[layer, step],
                    tile_peer(step),
                )
            )
            copies[-1].start()
        return copies

    def spread_members(layer):
        copies = []
        for step in range(1, members):
            other = lax.rem(member + step, members)
            copies.append(
                remote(
                    attz_buf.at[layer, pl.ds(other * own_rows, own_rows)],
                    fin_buf.at[layer, member],
                    fin_send.at[layer, step],
                    fin_recv.at[layer, step],
                    member_peer(step),
                )
            )
            copies[-1].start()
        return copies

    def project_out(layer, start, own_piece):
        total = start
        total = total + jnp.dot(
            own_piece, wout_buf[layer, member], preferred_element_type=jnp.float32
        )
        return total

    base = q_buf[pl.ds(tile_at * tile_rows, tile_rows)].astype(jnp.float32)
    final = q_buf[pl.ds(member * own_rows, own_rows)].astype(jnp.float32)
    pending = []
    for layer in range(layers):
        copies = attend(layer)
        if layer == 0:
            finish_item(1)
            for slot in range(slots):
                kv_copy(slot).wait_send()
        for hop in range(1, n_heads):
            if layer + 1 < layers:
                shares[2 + layer, hop].wait()
                start_relay(2 + layer, hop)
        if layer > 0:
            finish_item(1 + layer)
            own_w[layer].wait()
        merge(layer, copies)
        if layer + 1 < layers:
            mine = att_buf.at[layer, member]
            spread = []
            for step in range(1, members):
                spread.append(
                    remote(
                        mine,
                        mine,
                        att_send.at[layer, step],
                        att_recv.at[layer, step],
                        member_peer(step),
                    )
                )
                spread[-1].start()
            over_tiles = spread_tiles(layer)
            base = base + jnp.dot(
                att_buf[layer, member], wout_buf[layer, member], preferred_element_type=jnp.float32
            )
            for step in range(1, members):
                spread[step - 1].wait()
                other = lax.rem(member - step + members, members)
                base = base + jnp.dot(
                    att_buf[layer, other],
                    wout_buf[layer, other],
                    preferred_element_type=jnp.float32,
                )
            rows = pl.ds(tile_at * tile_rows, tile_rows)
            query_buf[layer + 1, rows] = to_query(base, layer + 1)
            gather = []
            for step in range(1, n_tiles):
                mine = query_buf.at[layer + 1, rows]
                gather.append(
                    remote(
                        mine,
                        mine,
                        qry_send.at[layer, step],
                        qry_recv.at[layer, step],
                        tile_peer(step),
                    )
                )
                gather[-1].start()
            for copy in over_tiles:
                copy.wait()
            pending.append(spread_members(layer))
            for copy in gather:
                copy.wait()
        else:
            over_tiles = spread_tiles(layer)
            for old, copies in enumerate(pending):
                own_piece = attz_buf[old, pl.ds(member * own_rows, own_rows)]
                final = project_out(old, final, own_piece)
                for step in range(1, members):
                    copies[step - 1].wait()
                    other = lax.rem(member - step + members, members)
                    final = final + jnp.dot(
                        fin_buf[old, other],
                        wout_buf[old, other],
                        preferred_element_type=jnp.float32,
                    )
            for copy in over_tiles:
                copy.wait()
            last = spread_members(layer)
            own_piece = attz_buf[layer, pl.ds(member * own_rows, own_rows)]
            final = project_out(layer, final, own_piece)
            for step in range(1, members):
                last[step - 1].wait()
                other = lax.rem(member - step + members, members)
                final = final + jnp.dot(
                    fin_buf[layer, other],
                    wout_buf[layer, other],
                    preferred_element_type=jnp.float32,
                )
            out_ref[...] = final


def fused_body(
    mesh, features, counts, tile_mask, queries, norm_gain, head_scale, w_query, w_kv, w_out
):
    n_tiles, n_heads, n_kv = (mesh.shape[name] for name in ("tiles", "heads", "kv"))
    members = n_heads * n_kv
    slots, block = tile_mask.shape
    own_rows, dq = queries.shape
    n_queries = own_rows * members
    tile_rows = n_queries // n_tiles
    layers, feat, _, side_cols = w_kv.shape
    cols = w_query.shape[2]
    own_heads = head_scale.shape[0] // n_kv
    head_dim = cols // own_heads
    width = -(-(cols + 2 * own_heads) // 128) * 128
    bf16, f32 = jnp.bfloat16, jnp.float32
    dma = pltpu.SemaphoreType.DMA
    any_spec = pl.BlockSpec(memory_space=pl.ANY)
    smem = pl.BlockSpec(memory_space=pltpu.SMEM)
    vmem = pl.BlockSpec(memory_space=pltpu.VMEM)
    return pl.pallas_call(
        functools.partial(fused_kernel, n_tiles, n_heads, n_kv),
        out_shape=jax.ShapeDtypeStruct((own_rows, dq), f32),
        in_specs=[smem, smem, vmem, vmem] + [any_spec] * 5,
        out_specs=vmem,
        scratch_shapes=[
            pltpu.VMEM((slots, block, feat), bf16),
            pltpu.VMEM((feat, layers * side_cols), bf16),
            pltpu.VMEM((layers, cols, dq), bf16),
            pltpu.VMEM((layers, members, cols, dq), bf16),
            pltpu.VMEM((n_queries, dq), bf16),
            pltpu.VMEM((slots, 2, layers, block, cols), bf16),
            pltpu.VMEM((slots, layers, block, cols), bf16),
            pltpu.VMEM((slots, block), f32),
            pltpu.VMEM((layers, n_queries, cols), bf16),
            pltpu.VMEM((own_heads, n_queries, head_dim), f32),
            pltpu.VMEM((own_heads, n_queries, 128), f32),
            pltpu.VMEM((layers, n_queries, width), bf16),
            pltpu.VMEM((layers, n_tiles, tile_rows, width), bf16),
            pltpu.VMEM((layers, members, tile_rows, cols), bf16),
            pltpu.VMEM((layers, n_queries, cols), bf16),
            pltpu.VMEM((layers, members, own_rows, cols), bf16),
            dma((layers + 1,)),
            dma((slots,)),
            dma((layers + 1,)),
            dma((layers + 1, n_heads)),
            dma((layers + 1, n_heads)),
            dma((layers + 1, n_heads)),
            dma((layers + 1, n_heads)),
            dma((slots,)),
            dma((slots,)),
            dma((layers, n_tiles)),
            dma((layers, n_tiles)),
            dma((layers, members)),
            dma((layers, members)),
            dma((layers, n_tiles)),
            dma((layers, n_tiles)),
            dma((layers, n_tiles)),
            dma((layers, n_tiles)),
            dma((layers, members)),
            dma((layers, members)),
        ],
        compiler_params=pltpu.CompilerParams(
            collective_id=0, has_side_effects=True, vmem_limit_bytes=56 * 1024 * 1024
        ),
    )(
        counts,
        head_scale,
        tile_mask,
        norm_gain,
        features,
        queries,
        jnp.swapaxes(w_query, 1, 2),
        w_kv.reshape(layers, feat, side_cols),
        w_out,
    )


def choose(mesh, *args):
    features, counts, tile_mask, queries, norm_gain, head_scale, w_query, w_kv, w_out = args
    n_tiles, n_heads, n_kv = (mesh.shape[name] for name in ("tiles", "heads", "kv"))
    n_queries = queries.shape[0] * n_heads * n_kv
    fits = (
        n_kv == 2
        and n_tiles > 1
        and n_heads > 1
        and head_scale.shape[0] % n_kv == 0
        and n_queries % (n_tiles * 16) == 0
        and queries.shape[0] % 16 == 0
        and tile_mask.shape[1] % 128 == 0
        and w_kv.shape[3] % 128 == 0
        and w_kv.shape[3] == n_kv * w_query.shape[2]
    )
    return fused_body(mesh, *args) if fits else body(*args)


def solution(mesh):
    return jax.shard_map(
        functools.partial(choose, mesh),
        mesh=mesh,
        in_specs=(
            P(("groups", "tiles"), None),
            P(("groups", "tiles")),
            P(("groups", "tiles"), None),
            P(("heads", "kv"), None),
            P(),
            P("heads"),
            P(None, None, ("heads", "kv")),
            P(None, None, "kv", "heads"),
            P(None, ("heads", "kv"), None),
        ),
        out_specs=P(("groups", "heads", "kv"), None),
        check_vma=False,
    )
```
